32 devices in a mesh: dp: 4 (over y, x), space: 8 (over z, core).
Axes of the slice: x: 2, y: 2, z: 4, core: 2. Of those that a mesh axis runs over, the one named last changes fastest.
Arguments:
- volume: bfloat16 [4, 64, 32, 2048], P('dp', None, 'space'), may hold values from -6 to 6
- conv_weight: bfloat16 [27, 64, 128], replicated, may hold values from -0.15625 to 0.15625
- mix_weight: bfloat16 [27, 128, 256], replicated, may hold values from -0.109375 to 0.109375
- cotangent: bfloat16 [4, 8, 256, 128], P('dp', 'space'), may hold values from -6 to 6
Outputs:
- mixed_out: bfloat16 [4, 8, 256, 128], P('dp', 'space')
- mix_grad: float32 [27, 128, 256], P(None, 'space')
The draws below stay inside these ranges and needn't reach their ends.
All inputs are finite; a program needn't handle non-finite values.
Results may differ from the reference program's by a relative error of at most 0.0049.
Values may be sent and summed in bfloat16 or wider, within the bound.
A program may use at most 64 MiB of HBM per device.

```python
import math
import jax
import jax.numpy as jnp
from jax import lax

C0 = 64
C1 = 128
C2 = 256
SY = 16
SZ = 128
BATCH = 4
XIN = 32
XOUT = 8
N_DP = 4


def block_scale(rng, extent, cuts, least, largest):
    factor_of = 1.0
    for dim, blocks in cuts:
        steps = jax.random.uniform(jax.random.fold_in(jax.random.fold_in(rng, 6), dim), (blocks,), jnp.float32, least / len(cuts), largest / len(cuts))
        factor_of = factor_of * jnp.repeat(jnp.exp(steps), extent[dim] // blocks).reshape((-1,) + (1,) * (len(extent) - 1 - dim))
    return factor_of


def gaussian(own_key, extent, spread, limit, split=(), dtype=jnp.bfloat16):
    level = block_scale(own_key, extent, split, -0.22, 0.18) if split else 1.0
    array = jax.random.normal(own_key, extent, jnp.float32) * spread * level
    return jnp.minimum(jnp.maximum(array, -limit), limit).astype(dtype)


def setup_inputs(seed: int = 0) -> dict:
    seeds = jax.random.split(jax.random.key(seed), 5)
    volume = gaussian(seeds[0], (BATCH, C0, XIN, SY * SZ), 1.0, 6.0, ((0, 4), (2, 8)))
    conv_weight = gaussian(seeds[1], (27, C0, C1), (27 * C0) ** -0.5, 0.15625)
    mix_weight = gaussian(seeds[2], (27, C1, C2), (27 * C1) ** -0.5, 0.109375)
    cotangent = gaussian(seeds[3], (BATCH, XOUT, C2, (SY // 4) * (SZ // 4)), 1.0, 6.0, ((0, 4), (1, 8)))
    return {"volume": volume, "conv_weight": conv_weight, "mix_weight": mix_weight, "cotangent": cotangent}


def conv_stride(volume, weights):
    kernel = weights.astype(jnp.float32).reshape(3, 3, 3, weights.shape[1], weights.shape[2])
    output = lax.conv_general_dilated(volume[None].astype(jnp.float32), kernel, (2, 2, 2), ((1, 1), (1, 1), (1, 1)), dimension_numbers=('NCDHW', 'DHWIO', 'NCDHW'), precision=lax.Precision.HIGHEST)
    return output[0]

def reference(volume, conv_weight, mix_weight, cotangent):

    def per_sample(grad_total, sample_pair):
        sample, cot_sample = sample_pair
        planes = sample.reshape(C0, XIN, SY, SZ)
        pre_act = conv_stride(planes, conv_weight)
        hidden = jnp.where(pre_act > 0, pre_act, 0.3 * pre_act).astype(jnp.bfloat16)
        hidden = lax.optimization_barrier(hidden)

        def forward(weights):
            return conv_stride(hidden, weights)
        output, pullback = jax.vjp(forward, mix_weight.astype(jnp.float32))
        cot_field = cot_sample.astype(jnp.float32).transpose(1, 0, 2).reshape(C2, XOUT, SY // 4, SZ // 4)
        gradient, = pullback(cot_field)
        result = output.astype(jnp.bfloat16).reshape(C2, XOUT, SY // 4 * (SZ // 4)).transpose(1, 0, 2)
        return (grad_total + gradient, result)
    initial = jnp.zeros((27, C1, C2), jnp.float32)
    grad_total, mixed_out = lax.scan(per_sample, initial, (volume, cotangent))
    scaling = 1.0 / math.sqrt(N_DP * XOUT * (SY // 4) * (SZ // 4))
    return (mixed_out, grad_total * scaling)
```

```python
import functools
import math

import jax
import jax.numpy as jnp
import numpy as np
from jax import lax
from jax.experimental import pallas as pl
from jax.experimental.pallas import tpu as pltpu
from jax.sharding import PartitionSpec as P

SY = 16
SZ = 128
JN = SY // 4
MN = SZ // 4
CELLS = JN * MN
ROWS = 16
MESH = pl.DeviceIdType.MESH


def up(value, step):
    return -(-value // step) * step


def selection():
    table = np.zeros((JN * SZ, 2, 5, JN, MN), np.float32)
    for shift in range(2):
        for v in range(5):
            for j in range(shift, JN):
                for m in range(MN):
                    z = 4 * m + v - 1
                    if z >= 0:
                        table[(j - shift) * SZ + z, shift, v, j, m] = 1.0
    return table.reshape(JN * SZ, 10 * CELLS)


def dot(a, b, dims):
    return lax.dot_general(a, b, (dims, ((), ())), preferred_element_type=jnp.float32)


def shift_m(value):
    lane = lax.broadcasted_iota(jnp.int32, value.shape, value.ndim - 1)
    return jnp.where(lane % MN == 0, 0.0, pltpu.roll(value, 1, value.ndim - 1))


def shift_j(value):
    lane = lax.broadcasted_iota(jnp.int32, value.shape, value.ndim - 1)
    return jnp.where(lane < MN, 0.0, pltpu.roll(value, MN, value.ndim - 1))


def windows(plane):
    parts = {}
    for r in range(2):
        even, odd = plane[2 * r], plane[2 * r + 1]
        odd_f = odd.astype(jnp.float32)
        before = shift_m(odd_f)
        parts[r + 1] = [before.astype(jnp.bfloat16), even, odd]
        if r == 1:
            parts[0] = [
                shift_j(before).astype(jnp.bfloat16),
                shift_j(even.astype(jnp.float32)).astype(jnp.bfloat16),
                shift_j(odd_f).astype(jnp.bfloat16),
            ]
    return parts[0] + parts[1] + parts[2]


def kernel(n, nd, scaling, vol, w1, w2, cot, sel, mixed, grad, halo, dmat, hid, rim, grp, cots, win, gsum, part, got,
           result, s_hv, s_hh, s_cot, r_cot, s_hid, r_hid, s_rs, r_rs, s_ag, r_ag):
    me = lax.axis_index("space")
    mine = lax.axis_index("dp")
    c1 = hid.shape[2]
    group = c1 // n
    span = max(group, ROWS)
    chunk = part.shape[0] // nd

    barrier = pltpu.get_barrier_semaphore()
    for d in range(1, n):
        pl.semaphore_signal(barrier, inc=1, device_id={"space": lax.rem(me + d, n)}, device_id_type=MESH)
    for d in range(1, nd):
        pl.semaphore_signal(barrier, inc=1, device_id={"dp": lax.rem(mine + d, nd)}, device_id_type=MESH)
    pl.semaphore_wait(barrier, n - 1 + nd - 1)

    above = lax.rem(me + 1, n)
    vol_copy = pltpu.make_async_remote_copy(
        vol.at[3], halo, s_hv.at[0], s_hv.at[1], device_id={"space": above}, device_id_type=MESH)
    rim_copy = pltpu.make_async_remote_copy(
        hid.at[1], rim, s_hh.at[0], s_hh.at[1], device_id={"space": above}, device_id_type=MESH)

    @pl.when(me < n - 1)
    def _():
        vol_copy.start()

    pending = []
    for d in range(1, n):
        copy = pltpu.make_async_remote_copy(
            cot, cots.at[d], s_cot.at[d], r_cot.at[d],
            device_id={"space": lax.rem(me + d, n)}, device_id_type=MESH)
        copy.start()
        pending.append(copy)

    def split(x, plane):
        rows = [
            jnp.concatenate([plane[:, (4 * j + s) * SZ : (4 * j + s + 1) * SZ] for j in range(JN)], axis=1)
            for s in range(4)
        ]
        c0 = plane.shape[0]
        flat = dot(jnp.concatenate(rows, axis=0), sel[:, : 5 * CELLS], ((1,), (0,))).astype(jnp.bfloat16)
        for s in range(4):
            dmat[x, s + 1] = flat[s * c0 : (s + 1) * c0]
        dmat[x, 0] = dot(rows[3], sel[:, 5 * CELLS :], ((1,), (0,))).astype(jnp.bfloat16)

    def first_layer(i):
        for r in range(2):
            stack = []
            for a in range(3):
                for b in range(3):
                    for c in range(3):
                        stack.append(jnp.concatenate(
                            [dmat[2 * i + a, 2 * r + b, :, v * CELLS : (v + 1) * CELLS] for v in (c, 2 + c)], axis=1))
            pre = dot(w1[...], jnp.concatenate(stack, axis=0), ((0,), (0,)))
            value = jnp.where(pre > 0, pre, 0.3 * pre).astype(jnp.bfloat16)
            for p in range(2):
                hid[i, 2 * r + p] = value[:, p * CELLS : (p + 1) * CELLS]

    def spread(i):
        for d in range(1, n):
            peer = lax.rem(me + d, n)
            start = pl.multiple_of((peer * group) // span * span, span)
            copy = pltpu.make_async_remote_copy(
                hid.at[i, :, pl.ds(start, span), :], grp.at[d, i], s_hid.at[i, d], r_hid.at[i, d],
                device_id={"space": peer}, device_id_type=MESH)
            copy.start()
            pending.append(copy)

    for x in (1, 2, 3):
        split(x + 1, vol[x])
    first_layer(1)

    @pl.when(me < n - 1)
    def _():
        rim_copy.start()

    spread(1)
    split(1, vol[0])

    @pl.when(me > 0)
    def _():
        vol_copy.wait_recv()

    @pl.when(me == 0)
    def _():
        halo[...] = jnp.zeros_like(halo)

    split(0, halo[...])
    first_layer(0)
    spread(0)

    @pl.when(me > 0)
    def _():
        rim_copy.wait_recv()

    @pl.when(me == 0)
    def _():
        rim[...] = jnp.zeros_like(rim)

    stack = []
    for plane in (rim, hid.at[0], hid.at[1]):
        stack += windows([plane[k] for k in range(4)])
    mixed[...] = dot(w2[...], jnp.concatenate(stack, axis=0), ((0,), (0,))).astype(jnp.bfloat16)

    for copy in pending:
        copy.wait_recv()
    own = pl.multiple_of((me * group) // span * span, span)
    grp[0] = hid[:, :, pl.ds(own, span), :]
    cots[0] = cot[...]
    for d in range(n):
        slab = lax.rem(me + n - d, n)
        last = windows([grp[d, 1, k] for k in range(4)])
        for k, value in enumerate(windows([grp[d, 0, k] for k in range(4)])):
            win[(9 + k) * span : (10 + k) * span, d * CELLS : (d + 1) * CELLS] = value
        for k, value in enumerate(last):
            win[(18 + k) * span : (19 + k) * span, d * CELLS : (d + 1) * CELLS] = value
        e = (d + n - 1) % n
        after = lax.rem(slab + 1, n)
        keep = jnp.where(after == 0, 0.0, 1.0)
        for k, value in enumerate(last):
            win[k * span : (k + 1) * span, e * CELLS : (e + 1) * CELLS] = (
                value.astype(jnp.float32) * keep).astype(jnp.bfloat16)
    cot_all = jnp.concatenate([cots[d] for d in range(n)], axis=1)
    total = dot(win[...], cot_all, ((1,), (1,))) * scaling
    used = total.shape[0]
    gsum[0:used] = total
    part[0:used] = total.astype(jnp.bfloat16)
    if used < part.shape[0]:
        gsum[used:] = jnp.zeros((part.shape[0] - used, total.shape[1]), jnp.float32)
        part[used:] = jnp.zeros((part.shape[0] - used, total.shape[1]), jnp.bfloat16)

    shares = []
    for d in range(1, nd):
        peer = lax.rem(mine + d, nd)
        copy = pltpu.make_async_remote_copy(
            part.at[pl.ds(pl.multiple_of(peer * chunk, ROWS), chunk)], got.at[d], s_rs.at[d], r_rs.at[d],
            device_id={"dp": peer}, device_id_type=MESH)
        copy.start()
        shares.append(copy)
    at = pl.multiple_of(mine * chunk, ROWS)
    value = gsum[pl.ds(at, chunk)]
    for d in range(1, nd):
        shares[d - 1].wait_recv()
        value = value + got[d].astype(jnp.float32)
    result[pl.ds(at, chunk)] = value.astype(jnp.bfloat16)
    gathers = []
    for d in range(1, nd):
        peer = lax.rem(mine + d, nd)
        copy = pltpu.make_async_remote_copy(
            result.at[pl.ds(at, chunk)], result.at[pl.ds(at, chunk)], s_ag.at[d], r_ag.at[d],
            device_id={"dp": peer}, device_id_type=MESH)
        copy.start()
        gathers.append(copy)
    for copy in gathers:
        copy.wait_recv()
    for k in range(27):
        grad[k] = result[k * span : (k + 1) * span].astype(jnp.float32)

    for copy in pending + shares + gathers:
        copy.wait_send()

    @pl.when(me < n - 1)
    def _():
        vol_copy.wait_send()
        rim_copy.wait_send()


def on_device(n, nd, volume, conv_weight, mix_weight, cotangent):
    c0, c1, c2 = volume.shape[1], conv_weight.shape[2], mix_weight.shape[2]
    group = c1 // n
    span = max(group, ROWS)
    scaling = 1.0 / math.sqrt(nd * n * cotangent.shape[1] * CELLS)
    used = 27 * span
    chunk = up(-(-used // nd), ROWS)
    vol = volume[0].transpose(1, 0, 2)
    sel = jnp.asarray(selection(), jnp.bfloat16)
    bf16, f32 = jnp.bfloat16, jnp.float32
    dma = pltpu.SemaphoreType.DMA
    mixed, grad = pl.pallas_call(
        functools.partial(kernel, n, nd, scaling),
        name="conv_pair",
        out_shape=(jax.ShapeDtypeStruct((c2, CELLS), bf16), jax.ShapeDtypeStruct((27, span, c2), f32)),
        in_specs=[pl.BlockSpec(memory_space=pltpu.VMEM)] * 5,
        out_specs=(pl.BlockSpec(memory_space=pltpu.VMEM),) * 2,
        scratch_shapes=[
            pltpu.VMEM((c0, SY * SZ), bf16),
            pltpu.VMEM((5, 5, c0, 5 * CELLS), bf16),
            pltpu.VMEM((2, 4, c1, CELLS), bf16),
            pltpu.VMEM((4, c1, CELLS), bf16),
            pltpu.VMEM((n, 2, 4, span, CELLS), bf16),
            pltpu.VMEM((n, c2, CELLS), bf16),
            pltpu.VMEM((used, n * CELLS), bf16),
            pltpu.VMEM((nd * chunk, c2), f32),
            pltpu.VMEM((nd * chunk, c2), bf16),
            pltpu.VMEM((nd, chunk, c2), bf16),
            pltpu.VMEM((nd * chunk, c2), bf16),
            dma((2,)), dma((2,)), dma((n,)), dma((n,)), dma((2, n)), dma((2, n)),
            dma((nd,)), dma((nd,)), dma((nd,)), dma((nd,)),
        ],
        compiler_params=pltpu.CompilerParams(collective_id=0, has_side_effects=True, vmem_limit_bytes=56 * 2**20),
    )(vol, conv_weight.reshape(27 * c0, c1), mix_weight.reshape(27 * c1, c2), cotangent[0, 0], sel)
    if span > group:
        grad = lax.dynamic_slice_in_dim(grad, lax.axis_index("space") * group % span, group, axis=1)
    return mixed[None, None], grad


def solution(mesh):
    return jax.shard_map(
        functools.partial(on_device, mesh.shape["space"], mesh.shape["dp"]),
        mesh=mesh,
        in_specs=(P("dp", None, "space", None), P(), P(), P("dp", "space", None, None)),
        out_specs=(P("dp", "space", None, None), P(None, "space", None)),
        check_vma=False,
    )
```

```python
import functools
import math

import jax
import jax.numpy as jnp
import numpy as np
from jax import lax
from jax.experimental import pallas as pl
from jax.experimental.pallas import tpu as pltpu
from jax.sharding import PartitionSpec as P

SY = 16
SZ = 128
JN = SY // 4
MN = SZ // 4
CELLS = JN * MN
ROWS = 16
MESH = pl.DeviceIdType.MESH


def up(value, step):
    return -(-value // step) * step


def selection():
    table = np.zeros((JN * SZ, 2, 5, JN, MN), np.float32)
    for shift in range(2):
        for v in range(5):
            for j in range(shift, JN):
                for m in range(MN):
                    z = 4 * m + v - 1
                    if z >= 0:
                        table[(j - shift) * SZ + z, shift, v, j, m] = 1.0
    return table.reshape(JN * SZ, 10 * CELLS)


def dot(a, b, dims):
    return lax.dot_general(a, b, (dims, ((), ())), preferred_element_type=jnp.float32)


def shift_m(value):
    lane = lax.broadcasted_iota(jnp.int32, value.shape, value.ndim - 1)
    return jnp.where(lane % MN == 0, 0.0, pltpu.roll(value, 1, value.ndim - 1))


def shift_j(value):
    lane = lax.broadcasted_iota(jnp.int32, value.shape, value.ndim - 1)
    return jnp.where(lane < MN, 0.0, pltpu.roll(value, MN, value.ndim - 1))


def windows(plane):
    parts = {}
    for r in range(2):
        even, odd = plane[2 * r], plane[2 * r + 1]
        odd_f = odd.astype(jnp.float32)
        before = shift_m(odd_f)
        parts[r + 1] = [before.astype(jnp.bfloat16), even, odd]
        if r == 1:
            parts[0] = [
                shift_j(before).astype(jnp.bfloat16),
                shift_j(even.astype(jnp.float32)).astype(jnp.bfloat16),
                shift_j(odd_f).astype(jnp.bfloat16),
            ]
    return parts[0] + parts[1] + parts[2]


def kernel(n, nd, scaling, vol_in, w1_in, w2_in, cot_in, sel_in, mixed, grad, vol, w1, w2, sel, halo, dmat, hid, rim, grp,
           cots, win, gsum, part, got, result, s_in, s_hv, s_hh, r_cot, s_cot, s_hid, r_hid, s_rs, r_rs, s_ag, r_ag):
    me = lax.axis_index("space")
    mine = lax.axis_index("dp")
    z, core = me // 2, me % 2
    chips = n // 2
    sibling = 2 * z + 1 - core
    c1 = hid.shape[2]
    group = c1 // n
    span = max(group, ROWS)

    loads = [
        pltpu.make_async_copy(src, dst, s_in.at[k])
        for k, (src, dst) in enumerate(
            ((vol_in, vol), (sel_in, sel), (w1_in, w1), (w2_in, w2), (cot_in, cots.at[me])))
    ]
    for load in loads:
        load.start()

    barrier = pltpu.get_barrier_semaphore()
    for d in range(1, n):
        pl.semaphore_signal(barrier, inc=1, device_id={"space": lax.rem(me + d, n)}, device_id_type=MESH)
    for d in range(1, nd):
        pl.semaphore_signal(barrier, inc=1, device_id={"dp": lax.rem(mine + d, nd)}, device_id_type=MESH)
    pl.semaphore_wait(barrier, n - 1 + nd - 1)

    above = lax.rem(me + 1, n)
    vol_copy = pltpu.make_async_remote_copy(
        vol_in.at[3], halo, s_hv.at[0], s_hv.at[1], device_id={"space": above}, device_id_type=MESH)
    rim_copy = pltpu.make_async_remote_copy(
        hid.at[1], rim, s_hh.at[0], s_hh.at[1], device_id={"space": above}, device_id_type=MESH)

    @pl.when(me < n - 1)
    def _():
        vol_copy.start()

    def cot_hop(block, source, target, way, h):
        return pltpu.make_async_remote_copy(
            block, cots.at[source], s_cot.at[way, h], r_cot.at[source],
            device_id={"space": target}, device_id_type=MESH)

    def relay(block, h, finish):
        act = (lambda copy: copy.wait_send()) if finish else (lambda copy: copy.start())
        lower, upper = (me + n - 2 * h) % n, (me + 2 * h) % n

        @pl.when(z >= h)
        def _():
            if h > 0 and not finish:
                cot_hop(block(lower), lower, sibling, 0, h).wait_recv()
            act(cot_hop(block(lower), lower, sibling, 0, h))

            @pl.when(z + 1 < chips)
            def _():
                act(cot_hop(block(lower), lower, (me + 2) % n, 1, h))

        @pl.when(z + h < chips)
        def _():
            if h > 0:
                if not finish:
                    cot_hop(block(upper), upper, sibling, 2, h).wait_recv()
                act(cot_hop(block(upper), upper, sibling, 2, h))

            @pl.when(z >= 1)
            def _():
                act(cot_hop(block(upper), upper, (me + n - 2) % n, 3, h))

    def block_of(h):
        return (lambda source: cot_in) if h == 0 else (lambda source: cots.at[source])

    relay(block_of(0), 0, False)

    def split(x, plane):
        rows = [
            jnp.concatenate([plane[:, (4 * j + s) * SZ : (4 * j + s + 1) * SZ] for j in range(JN)], axis=1)
            for s in range(4)
        ]
        c0 = plane.shape[0]
        flat = dot(jnp.concatenate(rows, axis=0), sel[:, : 5 * CELLS], ((1,), (0,))).astype(jnp.bfloat16)
        for s in range(4):
            dmat[x, s + 1] = flat[s * c0 : (s + 1) * c0]
        dmat[x, 0] = dot(rows[3], sel[:, 5 * CELLS :], ((1,), (0,))).astype(jnp.bfloat16)

    def first_layer(i):
        for r in range(2):
            stack = []
            for a in range(3):
                for b in range(3):
                    for c in range(3):
                        stack.append(jnp.concatenate(
                            [dmat[2 * i + a, 2 * r + b, :, v * CELLS : (v + 1) * CELLS] for v in (c, 2 + c)], axis=1))
            pre = dot(w1[...], jnp.concatenate(stack, axis=0), ((0,), (0,)))
            value = jnp.where(pre > 0, pre, 0.3 * pre).astype(jnp.bfloat16)
            for p in range(2):
                hid[i, 2 * r + p] = value[:, p * CELLS : (p + 1) * CELLS]

    own = pl.multiple_of((me * group) // span * span, span)

    def piece(i, d):
        peer = (me + d) % n
        start = pl.multiple_of((peer * group) // span * span, span)
        return pltpu.make_async_remote_copy(
            hid.at[i, :, pl.ds(start, span), :], grp.at[me, i], s_hid.at[i, d], r_hid.at[i, me],
            device_id={"space": peer}, device_id_type=MESH)

    def spread(i):
        for d in range(1, n):
            piece(i, d).start()
        grp[me, i] = hid[i, :, pl.ds(own, span), :]

    def collect(i):
        for d in range(1, n):
            source = (me + d) % n
            pltpu.make_async_remote_copy(
                hid.at[i, :, pl.ds(own, span), :], grp.at[source, i], s_hid.at[i, d], r_hid.at[i, source],
                device_id={"space": source}, device_id_type=MESH).wait_recv()

    loads[0].wait()
    loads[1].wait()
    for x in (1, 2, 3):
        split(x + 1, vol[x])
    loads[2].wait()
    first_layer(1)

    @pl.when(me < n - 1)
    def _():
        rim_copy.start()

    spread(1)
    split(1, vol[0])
    hops = list(range(1, chips))
    if hops:
        relay(block_of(1), 1, False)

    @pl.when(me > 0)
    def _():
        vol_copy.wait_recv()

    @pl.when(me == 0)
    def _():
        halo[...] = jnp.zeros_like(halo)

    split(0, halo[...])
    first_layer(0)
    spread(0)
    for h in hops[1:2]:
        relay(block_of(h), h, False)

    @pl.when(me > 0)
    def _():
        rim_copy.wait_recv()

    @pl.when(me == 0)
    def _():
        rim[...] = jnp.zeros_like(rim)

    stack = []
    for plane in (rim, hid.at[0], hid.at[1]):
        stack += windows([plane[k] for k in range(4)])
    loads[3].wait()
    mixed[...] = dot(w2[...], jnp.concatenate(stack, axis=0), ((0,), (0,))).astype(jnp.bfloat16)
    for h in hops[2:]:
        relay(block_of(h), h, False)

    def columns(s):
        return slice(s * CELLS, (s + 1) * CELLS)

    nine = 9 * span
    zero = jnp.zeros((span, CELLS), jnp.bfloat16)
    collect(1)
    for s in range(n):
        for k, value in enumerate(windows([grp[s, 1, q] for q in range(4)])):
            win[nine + k * span : nine + (k + 1) * span, columns(s)] = value
            if s < n - 1:
                win[k * span : (k + 1) * span, columns(s + 1)] = value
    for k in range(9):
        win[k * span : (k + 1) * span, columns(0)] = zero
    loads[4].wait()
    for d in range(chips):
        source = 2 * ((z + d) % chips) + 1 - core
        cot_hop(cots.at[source], source, sibling, 0, 0).wait_recv()
    cot_all = jnp.concatenate([cots[s] for s in range(n)], axis=1)

    bounds = (2 * nine, nine)
    chunks = [up(-(-bound // nd), ROWS) for bound in bounds]
    base = (0, nd * chunks[0])

    def share(t, d):
        peer = (mine + d) % nd
        at = pl.multiple_of(base[t] + peer * chunks[t], ROWS)
        return pltpu.make_async_remote_copy(
            part.at[pl.ds(at, chunks[t])], got.at[t, d, pl.ds(0, chunks[t])], s_rs.at[t, d], r_rs.at[t, d],
            device_id={"dp": peer}, device_id_type=MESH)

    def publish(t, d):
        at = pl.multiple_of(base[t] + mine * chunks[t], ROWS)
        return pltpu.make_async_remote_copy(
            result.at[pl.ds(at, chunks[t])], result.at[pl.ds(at, chunks[t])], s_ag.at[t, d], r_ag.at[t, d],
            device_id={"dp": (mine + d) % nd}, device_id_type=MESH)

    def total(t):
        first, count = (0, 2 * nine) if t == 0 else (2 * nine, nine)
        value = dot(win[first : first + count], cot_all, ((1,), (1,))) * scaling
        gsum[base[t] : base[t] + count] = value
        part[base[t] : base[t] + count] = value.astype(jnp.bfloat16)
        rest = nd * chunks[t] - count
        if rest:
            gsum[base[t] + count : base[t] + count + rest] = jnp.zeros((rest, value.shape[1]), jnp.float32)
            part[base[t] + count : base[t] + count + rest] = jnp.zeros((rest, value.shape[1]), jnp.bfloat16)
        for d in range(1, nd):
            share(t, d).start()

    def reduce(t):
        at = pl.multiple_of(base[t] + mine * chunks[t], ROWS)
        value = gsum[pl.ds(at, chunks[t])]
        for d in range(1, nd):
            share(t, d).wait_recv()
            value = value + got[t, d, : chunks[t]].astype(jnp.float32)
        result[pl.ds(at, chunks[t])] = value.astype(jnp.bfloat16)
        for d in range(1, nd):
            publish(t, d).start()

    total(0)
    collect(0)
    for s in range(n):
        for k, value in enumerate(windows([grp[s, 0, q] for q in range(4)])):
            win[2 * nine + k * span : 2 * nine + (k + 1) * span, columns(s)] = value
    total(1)
    reduce(0)
    reduce(1)
    for t, taps in ((0, [*range(9), *range(18, 27)]), (1, range(9, 18))):
        for d in range(1, nd):
            at = pl.multiple_of(base[t] + ((mine + nd - d) % nd) * chunks[t], ROWS)
            pltpu.make_async_remote_copy(
                result.at[pl.ds(at, chunks[t])], result.at[pl.ds(at, chunks[t])], s_ag.at[t, d], r_ag.at[t, d],
                device_id={"dp": (mine + d) % nd}, device_id_type=MESH).wait_recv()
        for k, tap in enumerate(taps):
            grad[tap] = result[base[t] + k * span : base[t] + (k + 1) * span].astype(jnp.float32)

    for i in range(2):
        for d in range(1, n):
            piece(i, d).wait_send()
        for d in range(1, nd):
            share(i, d).wait_send()
            publish(i, d).wait_send()
    for h in range(chips):
        relay(block_of(h), h, True)

    @pl.when(me < n - 1)
    def _():
        vol_copy.wait_send()
        rim_copy.wait_send()


def on_device(n, nd, volume, conv_weight, mix_weight, cotangent):
    c0, c1, c2 = volume.shape[1], conv_weight.shape[2], mix_weight.shape[2]
    group = c1 // n
    span = max(group, ROWS)
    scaling = 1.0 / math.sqrt(nd * n * cotangent.shape[1] * CELLS)
    used = 27 * span
    chunks = [up(-(-part // nd), ROWS) for part in (18 * span, 9 * span)]
    padded = nd * sum(chunks)
    vol = volume[0].transpose(1, 0, 2)
    sel = jnp.asarray(selection(), jnp.bfloat16)
    bf16, f32 = jnp.bfloat16, jnp.float32
    dma = pltpu.SemaphoreType.DMA
    mixed, grad = pl.pallas_call(
        functools.partial(kernel, n, nd, scaling),
        name="conv_pair",
        out_shape=(jax.ShapeDtypeStruct((c2, CELLS), bf16), jax.ShapeDtypeStruct((27, span, c2), f32)),
        in_specs=[pl.BlockSpec(memory_space=pl.ANY)] * 5,
        out_specs=(pl.BlockSpec(memory_space=pltpu.VMEM),) * 2,
        scratch_shapes=[
            pltpu.VMEM(vol.shape, bf16),
            pltpu.VMEM((27 * c0, c1), bf16),
            pltpu.VMEM((27 * c1, c2), bf16),
            pltpu.VMEM(sel.shape, bf16),
            pltpu.VMEM((c0, SY * SZ), bf16),
            pltpu.VMEM((5, 5, c0, 5 * CELLS), bf16),
            pltpu.VMEM((2, 4, c1, CELLS), bf16),
            pltpu.VMEM((4, c1, CELLS), bf16),
            pltpu.VMEM((n, 2, 4, span, CELLS), bf16),
            pltpu.VMEM((n, c2, CELLS), bf16),
            pltpu.VMEM((used, n * CELLS), bf16),
            pltpu.VMEM((padded, c2), f32),
            pltpu.VMEM((padded, c2), bf16),
            pltpu.VMEM((2, nd, chunks[0], c2), bf16),
            pltpu.VMEM((padded, c2), bf16),
            dma((5,)), dma((2,)), dma((2,)), dma((n,)), dma((4, n // 2)), dma((2, n)), dma((2, n)),
            dma((2, nd)), dma((2, nd)), dma((2, nd)), dma((2, nd)),
        ],
        compiler_params=pltpu.CompilerParams(collective_id=0, has_side_effects=True, vmem_limit_bytes=56 * 2**20),
    )(vol, conv_weight.reshape(27 * c0, c1), mix_weight.reshape(27 * c1, c2), cotangent[0, 0], sel)
    if span > group:
        grad = lax.dynamic_slice_in_dim(grad, lax.axis_index("space") * group % span, group, axis=1)
    return mixed[None, None], grad


def solution(mesh):
    return jax.shard_map(
        functools.partial(on_device, mesh.shape["space"], mesh.shape["dp"]),
        mesh=mesh,
        in_specs=(P("dp", None, "space", None), P(), P(), P("dp", "space", None, None)),
        out_specs=(P("dp", "space", None, None), P(None, "space", None)),
        check_vma=False,
    )
```
